32 devices in a mesh: parts: 2 (over x), blk: 16 (over z, y, core).
Axes of the slice: x: 2, y: 2, z: 4, core: 2. Of those that a mesh axis runs over, the one named last changes fastest.
Arguments:
- embeddings: bfloat16 [8192, 1024], P(('parts', 'blk')), parts along dimension 0, may hold values from -6 to 6
- cluster: int32 [8192, 1], P(('parts', 'blk')), parts along dimension 0, may hold values from 0 to 15; in each aligned block of 256 rows (0 to 255, 256 to 511, ...) at most 32 rows name the same one
- rank: int32 [8192], P(('parts', 'blk')), parts along dimension 0, may hold values from 0 to 4095, each once
Outputs:
- best: float32 [8192], P(('parts', 'blk')), parts along dimension 0
The draws below stay inside these ranges and needn't reach their ends.
There are 2 independent parts, one for each index of `parts`. The reference program is written for one: setup_inputs(seed, part) draws one part's arguments, and reference() takes and returns one part's arrays. A program takes and returns all parts, laid end to end along the dimension named above; each array names one. Nothing has to cross between parts.
Inputs may be any that keep to these rules, and one draw needn't show every extreme that they name: Cluster c is kept by index c of blk. The rows of one device name one cluster at most 32 times, a bound that some block reaches. Each rank appears once in a group.
All inputs are finite; a program needn't handle non-finite values.
Results may differ from the reference program's by a relative error of at most 0.0013.
Values may be sent and summed in bfloat16 or wider, within the bound.
No kernel may reach another device: no remote copies, remote signals or barrier semaphores. Data moves between devices by JAX's collectives and lax.ppermute only.
A program may use at most 64 MiB of HBM per device.

```python
import math
import jax
import jax.numpy as jnp
import numpy as np
from jax import lax

D = 1024
ROWS_DEV = 256
ROWS = 4096
CAP = 32
SLOTS = 512
N_BLK = 16


def levels(own_key, extent, split, least, top_value):
    level, own = 1.0, jax.random.fold_in(own_key, 6)
    for dim, parts in split:
        steps = jnp.exp(jax.random.uniform(jax.random.fold_in(own, dim), (parts,), jnp.float32, least / len(split), top_value / len(split)))
        level = level * jnp.repeat(steps, extent[dim] // parts).reshape([-1 if axis == dim else 1 for axis in range(len(extent))])
    return level


def assign_block(rng, own, number, rows, amount, top, most, skew):
    ranking = jax.random.permutation(rng, amount)
    heavy_load, ordinary = shares(amount, rows * top, most, skew, True), shares(amount, rows * top, most, skew, False)
    places = jnp.arange(amount)

    def named(tallies, turn):
        used = int((tallies > 0).sum())
        fixed = max(1, used // 4)
        moved = fixed + (places - fixed + turn * (used - fixed)) % max(1, amount - fixed)
        return jnp.zeros((amount,), jnp.int32).at[ranking[jnp.where(places < fixed, places, moved)]].set(jnp.asarray(tallies, jnp.int32))

    tallies = jnp.where(number % 4 == 0, named(heavy_load, number // 4), named(ordinary, number - number // 4 - 1))
    mixed = jax.random.permutation(jax.random.fold_in(own, 3), amount)
    donor, receiver = mixed[0:amount // 2 * 2:2], mixed[1:amount // 2 * 2:2]
    slack = jnp.minimum(tallies[donor] - 1, most - tallies[receiver]) // 2
    slack = jnp.where((donor == ranking[0]) | (receiver == ranking[0]) | (tallies[receiver] == 0), 0, jnp.maximum(slack, 0))
    moved = jax.random.randint(jax.random.fold_in(own, 4), (amount // 2,), 0, 1 << 20) % (slack + 1)
    tallies = tallies.at[donor].add(-moved).at[receiver].add(moved)
    items = jnp.searchsorted(jnp.cumsum(tallies), jnp.arange(rows * top), side="right").astype(jnp.int32)
    grid = items.reshape(top, rows).T
    grid = grid[jax.random.permutation(jax.random.fold_in(own, 1), rows)]
    turn = jax.random.randint(jax.random.fold_in(own, 2), (rows, 1), 0, top)
    return jnp.take_along_axis(grid, (jnp.arange(top)[None, :] + turn) % top, axis=1)


def shares(count, total, most, skew, full):
    loads = [(1 << 20) // math.isqrt(rank ** skew) + 1 for rank in range(1, count + 1)]
    largest = most if full else min(most, max(-(-total // count), total * loads[0] // sum(loads)))
    least = 1 if total - largest >= count - 1 else 0
    counts, surplus = [largest] + [least] * (count - 1), total - largest - least * (count - 1)
    while surplus > 0:
        candidates = [i for i in range(1, count) if counts[i] < largest] or [i for i in range(1, count) if counts[i] < most]
        pool, left = sum([loads[i] for i in candidates]), surplus
        for i in candidates:
            more = min(most - counts[i], max(1, left * loads[i] // pool), surplus)
            counts[i] = counts[i] + more
            surplus = surplus - more
    return np.array(counts)


def bell_draw(rng, extent, spread, reach, cuts=(), kind=jnp.bfloat16):
    loudness = levels(rng, extent, cuts, -0.22, 0.18) if cuts else 1.0
    drawn = jax.random.normal(rng, extent, jnp.float32) * spread * loudness
    return jnp.minimum(jnp.maximum(drawn, -reach), reach).astype(kind)


def setup_inputs(seed: int = 0, part: int = 0) -> dict:
    keys = jax.random.split(jax.random.key(seed), 4)
    own_keys = jax.random.split(jax.random.fold_in(keys[3], part), 4)
    embeddings = bell_draw(own_keys[0], (ROWS, D), 1.0, 6.0, ((0, 16),))
    cluster_keys = jax.random.split(jax.random.fold_in(own_keys[1], 1), ROWS // ROWS_DEV)
    cluster_turns = jax.random.permutation(jax.random.fold_in(own_keys[1], 3), ROWS // ROWS_DEV)
    cluster = jax.vmap(lambda own, number: assign_block(jax.random.fold_in(own_keys[1], 2), own, number, ROWS_DEV, N_BLK, 1, CAP, 2))(cluster_keys, cluster_turns).reshape((ROWS, 1))
    rank = jax.random.permutation(own_keys[2], ROWS).astype(jnp.int32)
    return {"embeddings": embeddings, "cluster": cluster, "rank": rank}


def reference(embeddings, cluster, rank):
    floats = embeddings.astype(jnp.float32)
    unit_rows = (floats * lax.rsqrt(lax.optimization_barrier(jnp.sum(floats * floats, axis=1, keepdims=True)) + 1e-06)).astype(jnp.bfloat16)
    labels = cluster[:, 0].astype(jnp.int32)
    grouping = jnp.argsort(labels, stable=True).astype(jnp.int32)
    grouped = unit_rows[grouping]
    group_rank = rank[grouping].astype(jnp.int32)
    group_ids = labels[grouping]
    counted = lax.optimization_barrier(jnp.sum((labels[:, None] == jnp.arange(N_BLK, dtype=jnp.int32)[None, :]).astype(jnp.int32), axis=0))
    starts = (jnp.cumsum(counted) - counted).astype(jnp.int32)
    padded_rows = jnp.concatenate([grouped, jnp.zeros((SLOTS, grouped.shape[1]), jnp.bfloat16)], axis=0)
    padded_rank = jnp.concatenate([group_rank, jnp.full((SLOTS,), -1, jnp.int32)], axis=0)
    padded_ids = jnp.concatenate([group_ids, jnp.full((SLOTS,), -1, jnp.int32)], axis=0)

    def one_cluster(which):
        begin_at = starts[which]
        window = lax.dynamic_slice_in_dim(padded_rows, begin_at, SLOTS, 0)
        win_rank = lax.dynamic_slice_in_dim(padded_rank, begin_at, SLOTS, 0)
        win_ids = lax.dynamic_slice_in_dim(padded_ids, begin_at, SLOTS, 0)
        similar = jnp.dot(window, window.T, preferred_element_type=jnp.float32)
        allowed = (win_ids[None, :] == which) & (win_rank[None, :] > win_rank[:, None])
        return lax.optimization_barrier(jnp.max(jnp.where(allowed, similar, -1.0), axis=1))
    results = lax.map(one_cluster, jnp.arange(N_BLK, dtype=jnp.int32))
    offsets = jnp.arange(ROWS, dtype=jnp.int32) - starts[group_ids]
    group_best = results[group_ids, offsets]
    return jnp.zeros((ROWS,), jnp.float32).at[grouping].set(group_best)
```

```python
import functools

import jax
import jax.numpy as jnp
from jax import lax
from jax.experimental import pallas as pl
from jax.experimental.pallas import tpu as pltpu
from jax.sharding import PartitionSpec as P

LANES = 128
TILE = 8


def prep_kernel(me_ref, emb_ref, cluster_ref, rank_ref, place_ref, *out_refs):
    devices = len(out_refs)
    rows, width = emb_ref.shape
    cap = 2 * rows // devices
    slots = devices * cap
    floats = emb_ref[...].astype(jnp.float32)
    unit = (floats * lax.rsqrt(jnp.sum(floats * floats, axis=1, keepdims=True) + 1e-06)).astype(jnp.bfloat16)
    cluster = cluster_ref[...]
    hot = lax.broadcasted_iota(jnp.int32, (devices, rows), 0) == cluster
    before = lax.broadcasted_iota(jnp.int32, (rows, rows), 0) < lax.broadcasted_iota(jnp.int32, (rows, rows), 1)
    earlier = jnp.dot(
        hot.astype(jnp.float32).astype(jnp.bfloat16),
        before.astype(jnp.float32).astype(jnp.bfloat16),
        preferred_element_type=jnp.float32,
    )
    within = jnp.sum(jnp.where(hot, earlier, 0.0), axis=0, keepdims=True).astype(jnp.int32)
    place_ref[...] = within
    slot = (cluster ^ me_ref[0]) * cap + within
    select = (lax.broadcasted_iota(jnp.int32, (slots, rows), 0) == slot).astype(jnp.float32).astype(jnp.bfloat16)
    placed = jnp.dot(select, unit, preferred_element_type=jnp.float32).astype(jnp.bfloat16)
    above = rank_ref[...] + 1
    line = lax.broadcasted_iota(jnp.int32, (TILE, rows), 0)
    digits = jnp.where(line == 0, above >> 8, jnp.where(line == 1, above & 255, 0))
    digit_slots = lax.dot_general(
        digits.astype(jnp.float32).astype(jnp.bfloat16),
        select,
        (((1,), (1,)), ((), ())),
        preferred_element_type=jnp.float32,
    )
    per = LANES // cap
    for d in range(devices):
        for j in range(width // LANES):
            out_refs[d][j * cap : (j + 1) * cap, :] = placed[d * cap : (d + 1) * cap, j * LANES : (j + 1) * LANES]
        lane = digit_slots[:, d // per * LANES : (d // per + 1) * LANES]
        if d % per:
            lane = pltpu.roll(lane, LANES - d % per * cap, 1)
        out_refs[d][cap * (width // LANES) :, :] = lane.astype(jnp.bfloat16)


def best_kernel(order, me_ref, *refs):
    out_ref, rows_ref = refs[-2:]
    block_refs = [ref for _, ref in sorted(zip(order, refs[:-2]), key=lambda pair: pair[0])]
    devices = len(block_refs)
    width = rows_ref.shape[1]
    slots = rows_ref.shape[0]
    cap = slots // devices
    per = LANES // cap
    ranks = []
    for d in range(devices):
        for j in range(width // LANES):
            rows_ref[d * cap : (d + 1) * cap, j * LANES : (j + 1) * LANES] = block_refs[d][j * cap : (j + 1) * cap, :]
        digits = block_refs[d][cap * (width // LANES) :, :].astype(jnp.float32)
        ranks.append(digits[0:1] * 256.0 + digits[1:2])
    rows = rows_ref[...]
    similar = lax.dot_general(rows, rows, (((1,), (1,)), ((), ())), preferred_element_type=jnp.float32)
    rank_lines = jnp.concatenate(ranks, axis=0)
    rank_down = jnp.transpose(rank_lines)
    key = jnp.concatenate([rank_down[:cap, d : d + 1] for d in range(devices)], axis=0)
    group = lax.broadcasted_iota(jnp.int32, (1, LANES), 1) // cap
    pieces = []
    for t in range(devices // per):
        piece = rank_lines[t * per : t * per + 1]
        for u in range(1, per):
            moved = pltpu.roll(rank_lines[t * per + u : t * per + u + 1], u * cap, 1)
            piece = jnp.where(group == u, moved, piece)
        pieces.append(piece)
    query = jnp.concatenate(pieces, axis=1)
    best = jnp.max(jnp.where(key > query, similar, -1.0), axis=0, keepdims=True)
    for d in range(devices):
        line = best[:, d // per * LANES : (d // per + 1) * LANES]
        if d % per:
            line = pltpu.roll(line, LANES - d % per * cap, 1)
        out_ref[me_ref[0] ^ d] = line


def pick_kernel(got_ref, cluster_ref, place_ref, out_ref):
    devices = got_ref.shape[0]
    rows = cluster_ref.shape[1]
    lines = jnp.concatenate([got_ref[c] for c in range(devices)], axis=0)
    hot = (lax.broadcasted_iota(jnp.int32, (LANES, rows), 0) == place_ref[...]).astype(jnp.float32)
    spread = jnp.dot(lines, hot, preferred_element_type=jnp.float32, precision=lax.Precision.HIGHEST)
    mine = lax.broadcasted_iota(jnp.int32, (devices, rows), 0) == cluster_ref[...]
    out_ref[...] = jnp.sum(jnp.where(mine, spread, 0.0), axis=0, keepdims=True)


def send_order(devices):
    half, quarter = devices // 2, devices // 4
    far = [half + i // 2 + (i % 2) * quarter for i in range(half)]
    near = list(range(quarter, half))
    order = [0]
    for i, d in enumerate(far):
        order.append(d)
        order += near[i : i + 1]
    return order + list(range(2, quarter)) + [1]


VMEM = pl.BlockSpec(memory_space=pltpu.VMEM)
SMEM = pl.BlockSpec(memory_space=pltpu.SMEM)


def local(embeddings, cluster, rank):
    devices = lax.axis_size("blk")
    rows, width = embeddings.shape
    cap = 2 * rows // devices
    slots = devices * cap
    me = lax.axis_index("blk").astype(jnp.int32).reshape(1)
    lines = cap * (width // LANES) + TILE
    cluster = cluster.reshape(1, rows)
    rank = rank.reshape(1, rows)
    block = pltpu.VMEM((lines, LANES), jnp.bfloat16)
    place, *send = pl.pallas_call(
        prep_kernel,
        in_specs=[SMEM, VMEM, VMEM, VMEM],
        out_specs=[VMEM] * (devices + 1),
        out_shape=[jax.ShapeDtypeStruct((1, rows), jnp.int32)] + [block] * devices,
        name="prep",
    )(me, embeddings, cluster, rank)
    order = send_order(devices)
    got = [send[0]]
    for d in order[1:]:
        moved = lax.ppermute(send[d], "blk", [(i, i ^ d) for i in range(devices)])
        got.append(pltpu.with_memory_space_constraint(moved, pltpu.VMEM))
    best = pl.pallas_call(
        functools.partial(best_kernel, order),
        in_specs=[SMEM] + [VMEM] * devices,
        out_specs=VMEM,
        out_shape=jax.ShapeDtypeStruct((devices, 1, LANES), jnp.float32),
        scratch_shapes=[pltpu.VMEM((slots, width), jnp.bfloat16)],
        name="best",
    )(me, *got)
    back = lax.all_to_all(best, "blk", split_axis=0, concat_axis=0, tiled=True)
    out = pl.pallas_call(
        pick_kernel,
        in_specs=[VMEM] * 3,
        out_specs=VMEM,
        out_shape=jax.ShapeDtypeStruct((1, rows), jnp.float32),
        name="pick",
    )(back, cluster, place)
    return out.reshape(rows)


def best_over(q_rows, q_rank, k_rows, k_rank):
    similar = lax.dot_general(q_rows, k_rows, (((1,), (1,)), ((), ())), preferred_element_type=jnp.float32)
    allowed = k_rank[None, :] > q_rank[:, None]
    return jnp.max(jnp.where(allowed, similar, -1.0), axis=1)


def local_plain(embeddings, cluster, rank):
    devices = lax.axis_size("blk")
    rows, width = embeddings.shape
    slots = 2 * rows
    cap = slots // devices
    floats = embeddings.astype(jnp.float32)
    unit = (floats * lax.rsqrt(jnp.sum(floats * floats, axis=1, keepdims=True) + 1e-06)).astype(jnp.bfloat16)
    target = cluster[:, 0]
    hot = (target[:, None] == jnp.arange(devices, dtype=jnp.int32)[None, :]).astype(jnp.int32)
    within = jnp.sum((jnp.cumsum(hot, axis=0) - hot) * hot, axis=1)
    slot_of = target * cap + within
    send_rows = jnp.zeros((slots, width), jnp.bfloat16).at[slot_of].set(unit).reshape(devices, cap, width)
    send_rank = jnp.full((slots,), -1, jnp.int32).at[slot_of].set(rank).reshape(devices, cap)
    got_rows = lax.all_to_all(send_rows, "blk", split_axis=0, concat_axis=0, tiled=True).reshape(slots, width)
    got_rank = lax.all_to_all(send_rank, "blk", split_axis=0, concat_axis=0, tiled=True).reshape(slots)
    best = best_over(got_rows, got_rank, got_rows, got_rank).reshape(devices, cap)
    back = lax.all_to_all(best, "blk", split_axis=0, concat_axis=0, tiled=True)
    return back.reshape(slots)[slot_of]


def solution(mesh):
    devices = mesh.shape["blk"]

    def step(embeddings, cluster, rank):
        rows = embeddings.shape[0] // mesh.size
        cap = 2 * rows // devices
        tiled = cap % 16 == 0 and LANES % cap == 0 and devices & (devices - 1) == 0 and embeddings.shape[1] % LANES == 0
        tiled = tiled and rows * devices < 65536 and devices % (LANES // max(cap, 1)) == 0
        return jax.shard_map(
            local if tiled else local_plain,
            mesh=mesh,
            in_specs=(P(("parts", "blk"), None), P(("parts", "blk"), None), P(("parts", "blk"))),
            out_specs=P(("parts", "blk")),
            check_vma=False,
        )(embeddings, cluster, rank)

    return step
```

```python
import functools

import jax
import jax.numpy as jnp
from jax import lax
from jax.experimental import pallas as pl
from jax.experimental.pallas import tpu as pltpu
from jax.sharding import PartitionSpec as P

LANES = 128
LANE_BITS = 7
TILE = 8


def write_blocks(placed, digit_slots, which, cap, out_refs):
    width = placed.shape[1]
    per = LANES // cap
    for i, (d, out_ref) in enumerate(zip(which, out_refs)):
        for j in range(width // LANES):
            out_ref[j * cap : (j + 1) * cap, :] = placed[i * cap : (i + 1) * cap, j * LANES : (j + 1) * LANES]
        lane = digit_slots[:, d // per * LANES : (d // per + 1) * LANES]
        if d % per:
            lane = pltpu.roll(lane, LANES - d % per * cap, 1)
        out_ref[cap * (width // LANES) :, :] = lane.astype(jnp.bfloat16)


def one_hot(slots, slot):
    lines = lax.broadcasted_iota(jnp.int32, (slots, slot.shape[1]), 0)
    return (lines == slot).astype(jnp.float32).astype(jnp.bfloat16)


def rank_digits(rank):
    above = rank + 1
    line = lax.broadcasted_iota(jnp.int32, (TILE, rank.shape[1]), 0)
    digits = jnp.where(line == 0, above >> 8, jnp.where(line == 1, above & 255, 0))
    return digits.astype(jnp.float32).astype(jnp.bfloat16)


def place(select, rows, digits):
    placed = jnp.dot(select, rows, preferred_element_type=jnp.float32).astype(jnp.bfloat16)
    return placed, lax.dot_general(digits, select, (((1,), (1,)), ((), ())), preferred_element_type=jnp.float32)


def prep_kernel(first, cap, me_ref, emb_ref, cluster_ref, rank_ref, code_ref, slot_ref, unit_ref, digits_ref, *out_refs):
    rows, width = emb_ref.shape
    devices = 2 * rows // cap
    floats = emb_ref[...].astype(jnp.float32)
    unit = (floats * lax.rsqrt(jnp.sum(floats * floats, axis=1, keepdims=True) + 1e-06)).astype(jnp.bfloat16)
    unit_ref[...] = unit
    cluster = cluster_ref[...]
    hot = lax.broadcasted_iota(jnp.int32, (devices, rows), 0) == cluster
    before = lax.broadcasted_iota(jnp.int32, (rows, rows), 0) < lax.broadcasted_iota(jnp.int32, (rows, rows), 1)
    earlier = jnp.dot(
        hot.astype(jnp.float32).astype(jnp.bfloat16),
        before.astype(jnp.float32).astype(jnp.bfloat16),
        preferred_element_type=jnp.float32,
    )
    within = jnp.sum(jnp.where(hot, earlier, 0.0), axis=0, keepdims=True).astype(jnp.int32)
    code_ref[...] = (cluster << LANE_BITS) + within
    slot = (cluster ^ me_ref[0]) * cap + within
    slot_ref[...] = slot
    digits = rank_digits(rank_ref[...])
    digits_ref[...] = digits
    per = LANES // cap
    for d, out_ref in zip(first, out_refs):
        group = one_hot(LANES, slot - d // per * LANES)
        placed, digit_slots = place(group, unit, digits)
        i = d % per
        write_blocks(placed[i * cap : (i + 1) * cap], digit_slots, [i], cap, [out_ref])


def rest_kernel(rest, cap, slot_ref, unit_ref, digits_ref, *out_refs):
    slot = slot_ref[...]
    unit = unit_ref[...]
    digits = digits_ref[...]
    per = LANES // cap
    for t in range(0, 2 * unit.shape[0] // cap, per):
        placed, digit_slots = place(one_hot(LANES, slot - t * cap), unit, digits)
        for d in rest:
            if t <= d < t + per:
                i = d - t
                write_blocks(placed[i * cap : (i + 1) * cap], digit_slots, [i], cap, [out_refs[rest.index(d)]])


def best_kernel(order, me_ref, *refs):
    out_ref, rows_ref = refs[-2:]
    block_refs = [ref for _, ref in sorted(zip(order, refs[:-2]), key=lambda pair: pair[0])]
    devices = len(block_refs)
    width = rows_ref.shape[1]
    slots = rows_ref.shape[0]
    cap = slots // devices
    per = LANES // cap
    ranks = []
    for d in range(devices):
        for j in range(width // LANES):
            rows_ref[d * cap : (d + 1) * cap, j * LANES : (j + 1) * LANES] = block_refs[d][j * cap : (j + 1) * cap, :]
        digits = block_refs[d][cap * (width // LANES) :, :].astype(jnp.float32)
        ranks.append(digits[0:1] * 256.0 + digits[1:2])
    rows = rows_ref[...]
    similar = lax.dot_general(rows, rows, (((1,), (1,)), ((), ())), preferred_element_type=jnp.float32)
    rank_lines = jnp.concatenate(ranks, axis=0)
    rank_down = jnp.transpose(rank_lines)
    key = jnp.concatenate([rank_down[:cap, d : d + 1] for d in range(devices)], axis=0)
    group = lax.broadcasted_iota(jnp.int32, (1, LANES), 1) // cap
    pieces = []
    for t in range(devices // per):
        piece = rank_lines[t * per : t * per + 1]
        for u in range(1, per):
            moved = pltpu.roll(rank_lines[t * per + u : t * per + u + 1], u * cap, 1)
            piece = jnp.where(group == u, moved, piece)
        pieces.append(piece)
    query = jnp.concatenate(pieces, axis=1)
    best = jnp.max(jnp.where(key > query, similar, -1.0), axis=0, keepdims=True)
    for d in range(devices):
        line = best[:, d // per * LANES : (d // per + 1) * LANES]
        if d % per:
            line = pltpu.roll(line, LANES - d % per * cap, 1)
        out_ref[me_ref[0] ^ d] = line


def pick_kernel(got_ref, code_ref, out_ref):
    devices = got_ref.shape[0]
    rows = code_ref.shape[1]
    lines = jnp.concatenate([got_ref[c] for c in range(devices)], axis=0)
    for t in range(rows // LANES):
        code = code_ref[:, t * LANES : (t + 1) * LANES]
        place = jnp.broadcast_to(code & (LANES - 1), (devices, LANES))
        spread = jnp.take_along_axis(lines, place, axis=1)
        mine = lax.broadcasted_iota(jnp.int32, (devices, LANES), 0) == code >> LANE_BITS
        out_ref[:, t * LANES : (t + 1) * LANES] = jnp.sum(jnp.where(mine, spread, 0.0), axis=0, keepdims=True)


def send_order(devices):
    half, quarter = devices // 2, devices // 4
    far = [half + i // 2 + (i % 2) * quarter for i in range(half)]
    near = [*range(quarter, half), *range(2, quarter), 1]
    order = [0, far[0]]
    for d, e in zip(far[1:], near):
        order += [d, e]
    return order


def in_vmem(x):
    return pltpu.with_memory_space_constraint(x, pltpu.VMEM)


VMEM = pl.BlockSpec(memory_space=pltpu.VMEM)
SMEM = pl.BlockSpec(memory_space=pltpu.SMEM)


def local(embeddings, cluster, rank):
    devices = lax.axis_size("blk")
    rows, width = embeddings.shape
    cap = 2 * rows // devices
    slots = devices * cap
    me = lax.axis_index("blk").astype(jnp.int32).reshape(1)
    lines = cap * (width // LANES) + TILE
    order = send_order(devices)
    first = order[1:2]
    rest = [d for d in range(devices) if d not in first]
    block = pltpu.VMEM((lines, LANES), jnp.bfloat16)
    code, slot, unit, digits, *head = pl.pallas_call(
        functools.partial(prep_kernel, first, cap),
        in_specs=[SMEM, VMEM, VMEM, VMEM],
        out_specs=[VMEM] * (4 + len(first)),
        out_shape=[
            pltpu.VMEM((1, rows), jnp.int32),
            pltpu.VMEM((1, rows), jnp.int32),
            pltpu.VMEM((rows, width), jnp.bfloat16),
            pltpu.VMEM((TILE, rows), jnp.bfloat16),
        ]
        + [block] * len(first),
        name="prep",
    )(me, embeddings, cluster.reshape(1, rows), rank.reshape(1, rows))
    tail = pl.pallas_call(
        functools.partial(rest_kernel, rest, cap),
        in_specs=[VMEM] * 3,
        out_specs=[VMEM] * len(rest),
        out_shape=[block] * len(rest),
        name="rest",
    )(in_vmem(slot), in_vmem(unit), in_vmem(digits))
    send = dict(zip(first + rest, [*head, *tail]))
    got = [in_vmem(send[0])]
    for d in order[1:]:
        moved = lax.ppermute(send[d], "blk", [(i, i ^ d) for i in range(devices)])
        got.append(in_vmem(moved))
    best = pl.pallas_call(
        functools.partial(best_kernel, order),
        in_specs=[SMEM] + [VMEM] * devices,
        out_specs=VMEM,
        out_shape=pltpu.VMEM((devices, 1, LANES), jnp.float32),
        scratch_shapes=[pltpu.VMEM((slots, width), jnp.bfloat16)],
        name="best",
    )(me, *got)
    back = lax.all_to_all(best, "blk", split_axis=0, concat_axis=0, tiled=True)
    out = pl.pallas_call(
        pick_kernel,
        in_specs=[VMEM] * 2,
        out_specs=VMEM,
        out_shape=jax.ShapeDtypeStruct((1, rows), jnp.float32),
        name="pick",
    )(in_vmem(back), in_vmem(code))
    return out.reshape(rows)


def best_over(q_rows, q_rank, k_rows, k_rank):
    similar = lax.dot_general(q_rows, k_rows, (((1,), (1,)), ((), ())), preferred_element_type=jnp.float32)
    allowed = k_rank[None, :] > q_rank[:, None]
    return jnp.max(jnp.where(allowed, similar, -1.0), axis=1)


def local_plain(embeddings, cluster, rank):
    devices = lax.axis_size("blk")
    rows, width = embeddings.shape
    slots = 2 * rows
    cap = slots // devices
    floats = embeddings.astype(jnp.float32)
    unit = (floats * lax.rsqrt(jnp.sum(floats * floats, axis=1, keepdims=True) + 1e-06)).astype(jnp.bfloat16)
    target = cluster[:, 0]
    hot = (target[:, None] == jnp.arange(devices, dtype=jnp.int32)[None, :]).astype(jnp.int32)
    within = jnp.sum((jnp.cumsum(hot, axis=0) - hot) * hot, axis=1)
    slot_of = target * cap + within
    send_rows = jnp.zeros((slots, width), jnp.bfloat16).at[slot_of].set(unit).reshape(devices, cap, width)
    send_rank = jnp.full((slots,), -1, jnp.int32).at[slot_of].set(rank).reshape(devices, cap)
    got_rows = lax.all_to_all(send_rows, "blk", split_axis=0, concat_axis=0, tiled=True).reshape(slots, width)
    got_rank = lax.all_to_all(send_rank, "blk", split_axis=0, concat_axis=0, tiled=True).reshape(slots)
    best = best_over(got_rows, got_rank, got_rows, got_rank).reshape(devices, cap)
    back = lax.all_to_all(best, "blk", split_axis=0, concat_axis=0, tiled=True)
    return back.reshape(slots)[slot_of]


def solution(mesh):
    devices = mesh.shape["blk"]

    def step(embeddings, cluster, rank):
        rows = embeddings.shape[0] // mesh.size
        cap = 2 * rows // devices
        tiled = cap % 16 == 0 and LANES % cap == 0 and devices & (devices - 1) == 0 and embeddings.shape[1] % LANES == 0
        tiled = tiled and rows % LANES == 0 and rows * devices < 65536 and devices % (LANES // max(cap, 1)) == 0
        return jax.shard_map(
            local if tiled else local_plain,
            mesh=mesh,
            in_specs=(P(("parts", "blk"), None), P(("parts", "blk"), None), P(("parts", "blk"))),
            out_specs=P(("parts", "blk")),
            check_vma=False,
        )(embeddings, cluster, rank)

    return step
```
